32 devices in a mesh: dp: 4 (over y, x), expert: 8 (over z, core).
Axes of the slice: x: 2, y: 2, z: 4, core: 2. Of those that a mesh axis runs over, the one named last changes fastest.
Arguments:
- tokens: bfloat16 [1024, 7168], P('expert', 'dp'), may hold values from -6 to 6
- cotangent: bfloat16 [1024, 7168], P('expert', 'dp'), may hold values from -6 to 6
- routes: int32 [1024, 4], P('expert'), may hold values from 0 to 7, all different within a row; in each aligned block of 128 rows (0 to 127, 128 to 255, ...) at most 96 rows name the same one
- gates: float32 [1024, 4], P('expert'), may hold values from 0.2 to 1
- w_gate: bfloat16 [8, 7168, 1024], P('expert', 'dp'), may hold values from -0.0625 to 0.0625
- w_up: bfloat16 [8, 7168, 1024], P('expert', 'dp'), may hold values from -0.0625 to 0.0625
- w_down: bfloat16 [8, 1024, 7168], P('expert', None, 'dp'), may hold values from -0.1875 to 0.1875
Outputs:
- mixed: bfloat16 [1024, 7168], P('expert', 'dp')
- input_grad: bfloat16 [1024, 7168], P('expert', 'dp')
- grad_w_gate: bfloat16 [8, 7168, 1024], P('expert', 'dp')
- grad_w_up: bfloat16 [8, 7168, 1024], P('expert', 'dp')
- grad_w_down: bfloat16 [8, 1024, 7168], P('expert', None, 'dp')
The draws below stay inside these ranges and needn't reach their ends.
Inputs may be any that keep to these rules, and one draw needn't show every extreme that they name: `routes`: A row names 4 different experts; in each aligned block of 128 rows (the tokens of one index of expert) no expert is named by more than 96 rows, a bound that some block reaches.
All inputs are finite; a program needn't handle non-finite values.
Results may differ from the reference program's by a relative error of at most 0.019.
Values may be sent and summed in bfloat16 or wider, within the bound.
No kernel may reach another device: no remote copies, remote signals or barrier semaphores. Data moves between devices by JAX's collectives and lax.ppermute only.
A program may use at most 128 MiB of HBM per device.

```python
import math
import jax
import jax.numpy as jnp
import numpy as np
from jax import lax

D = 7168
H = 1024
TOP = 4
TOK_DEV = 128
EXPERTS = 8
TOKENS = 1024
CAP = 96
ROWS = 768
D_PART = 1792
N_DP = 4
N_EXPERT = 8


def steps_of(own_key, shape, pieces, smallest, top_value):
    def one(axis_at, parts):
        steps = jax.random.uniform(jax.random.fold_in(jax.random.fold_in(own_key, 6), axis_at), (parts,), jnp.float32, smallest / len(pieces), top_value / len(pieces))
        return jnp.repeat(jnp.exp(steps), shape[axis_at] // parts).reshape((-1,) + (1,) * (len(shape) - axis_at - 1))

    gain = one(*pieces[0])
    for cut in pieces[1:]:
        gain = gain * one(*cut)
    return gain


def assign_block(own_key, own, number, rows, count, top, limit, skew):
    sequence = jax.random.permutation(own_key, count)
    packed, usual = portions_of(count, rows * top, limit, skew, True), portions_of(count, rows * top, limit, skew, False)
    places = jnp.arange(count)

    def named(sizes, turn):
        used = int((sizes > 0).sum())
        fixed = max(1, used // 4)
        shifted = fixed + (places - fixed + turn * (used - fixed)) % max(1, count - fixed)
        return jnp.zeros((count,), jnp.int32).at[sequence[jnp.where(places < fixed, places, shifted)]].set(jnp.asarray(sizes, jnp.int32))

    sizes = jnp.where(number % 4 == 0, named(packed, number // 4), named(usual, number - number // 4 - 1))
    mixed = jax.random.permutation(jax.random.fold_in(own, 3), count)
    donor, sink = mixed[0:count // 2 * 2:2], mixed[1:count // 2 * 2:2]
    room = jnp.minimum(sizes[donor] - 1, limit - sizes[sink]) // 2
    room = jnp.where((donor == sequence[0]) | (sink == sequence[0]) | (sizes[sink] == 0), 0, jnp.maximum(room, 0))
    shifted = jax.random.randint(jax.random.fold_in(own, 4), (count // 2,), 0, 1 << 20) % (room + 1)
    sizes = sizes.at[donor].add(-shifted).at[sink].add(shifted)
    labels = jnp.searchsorted(jnp.cumsum(sizes), jnp.arange(rows * top), side="right").astype(jnp.int32)
    table = labels.reshape(top, rows).T
    table = table[jax.random.permutation(jax.random.fold_in(own, 1), rows)]
    turn = jax.random.randint(jax.random.fold_in(own, 2), (rows, 1), 0, top)
    return jnp.take_along_axis(table, (jnp.arange(top)[None, :] + turn) % top, axis=1)


def portions_of(number_of, total, most, lean, full):
    loads = [(1 << 20) // math.isqrt(rank ** lean) + 1 for rank in range(1, number_of + 1)]
    largest = most if full else min(most, max(-(-total // number_of), total * loads[0] // sum(loads)))
    least = 1 if total - largest >= number_of - 1 else 0
    given, surplus = [largest] + [least] * (number_of - 1), total - largest - least * (number_of - 1)
    while surplus > 0:
        candidates = [i for i in range(1, number_of) if given[i] < largest] or [i for i in range(1, number_of) if given[i] < most]
        mass, remaining = sum([loads[i] for i in candidates]), surplus
        for i in candidates:
            more = min(most - given[i], max(1, remaining * loads[i] // mass), surplus)
            given[i] = given[i] + more
            surplus = surplus - more
    return np.array(given)


def scatter_about(stream_key, dims, scale, bound, pieces=(), kind=jnp.bfloat16):
    result = jax.random.normal(stream_key, dims, jnp.float32) * scale
    if len(pieces) > 0:
        result = steps_of(stream_key, dims, pieces, -0.22, 0.18) * result
    return jnp.clip(result, min=-bound, max=bound).astype(kind)


def setup_inputs(seed: int = 0) -> dict:
    seeds = jax.random.split(jax.random.key(seed), 8)
    tokens = scatter_about(seeds[0], (TOKENS, D), 1.0, 6.0, ((0, 8), (1, 4)))
    cotangent = scatter_about(seeds[1], (TOKENS, D), 1.0, 6.0, ((0, 8), (1, 4)))
    routes_keys = jax.random.split(jax.random.fold_in(seeds[2], 1), TOKENS // TOK_DEV)
    routes_turns = jax.random.permutation(jax.random.fold_in(seeds[2], 3), TOKENS // TOK_DEV)
    routes = jax.vmap(lambda own, number: assign_block(jax.random.fold_in(seeds[2], 2), own, number, TOK_DEV, EXPERTS, TOP, CAP, 2))(routes_keys, routes_turns).reshape((TOKENS, TOP))
    gates = jnp.clip(0.2 + 0.8 * jax.random.uniform(seeds[3], (TOKENS, TOP), jnp.float32) ** steps_of(seeds[3], (TOKENS, TOP), ((0, 8),), -0.2, 0.2), 0.2, 1.0)
    w_gate = scatter_about(seeds[4], (EXPERTS, D, H), D ** -0.5, 0.0625, ((0, 8), (1, 4)))
    w_up = scatter_about(seeds[5], (EXPERTS, D, H), D ** -0.5, 0.0625, ((0, 8), (1, 4)))
    w_down = scatter_about(seeds[6], (EXPERTS, H, D), H ** -0.5, 0.1875, ((0, 8), (2, 4)))
    return {"tokens": tokens, "cotangent": cotangent, "routes": routes, "gates": gates, "w_gate": w_gate, "w_up": w_up, "w_down": w_down}


def block_ranks(picks):
    onehot = (picks[:, None] == jnp.arange(EXPERTS, dtype=jnp.int32)[None, :]).astype(jnp.int32)
    before = jnp.cumsum(onehot, axis=0) - onehot
    return jnp.sum(before * onehot, axis=1).astype(jnp.int32)


def part_sum(left_rows, weight):
    count = left_rows.shape[0]
    left_parts = left_rows.reshape(count, N_DP, D_PART).astype(jnp.float32)
    weight_parts = weight.reshape(N_DP, D_PART, weight.shape[1]).astype(jnp.float32)
    partial_value = jnp.einsum("rqd,qdh->rqh", left_parts, weight_parts)
    rounded = lax.optimization_barrier(partial_value.astype(jnp.bfloat16))
    return jnp.sum(rounded.astype(jnp.float32), axis=1)


def expert_work(operands):
    expert_x, expert_d, weight_gate, weight_up, weight_down = operands
    gate_pre = part_sum(expert_x, weight_gate)
    up_pre = part_sum(expert_x, weight_up)
    hidden = (jax.nn.silu(gate_pre) * up_pre).astype(jnp.bfloat16)
    out_rows = jnp.dot(hidden, weight_down, preferred_element_type=jnp.float32).astype(jnp.bfloat16)
    hidden_grad = part_sum(expert_d, weight_down.T)
    gate_sig = jax.nn.sigmoid(gate_pre)
    gate_grad = (hidden_grad * up_pre * gate_sig * (1.0 + gate_pre * (1.0 - gate_sig))).astype(jnp.bfloat16)
    up_grad = (hidden_grad * gate_pre * gate_sig).astype(jnp.bfloat16)
    row_grads = (jnp.dot(gate_grad, weight_gate.T, preferred_element_type=jnp.float32)
                 + jnp.dot(up_grad, weight_up.T, preferred_element_type=jnp.float32)).astype(jnp.bfloat16)
    grad_gate = jnp.dot(expert_x.T, gate_grad, preferred_element_type=jnp.float32).astype(jnp.bfloat16)
    grad_up = jnp.dot(expert_x.T, up_grad, preferred_element_type=jnp.float32).astype(jnp.bfloat16)
    grad_down = jnp.dot(hidden.T, expert_d, preferred_element_type=jnp.float32).astype(jnp.bfloat16)
    return out_rows, row_grads, grad_gate, grad_up, grad_down


def reference(tokens, cotangent, routes, gates, w_gate, w_up, w_down):
    picks = routes.reshape(N_EXPERT, TOK_DEV * TOP)
    slot_rank = jax.vmap(block_ranks)(picks).reshape(-1)
    expert_of = routes.reshape(-1).astype(jnp.int32)
    token_of = (jnp.arange(TOKENS * TOP, dtype=jnp.int32) // TOP).astype(jnp.int32)
    row_of = ((token_of // TOK_DEV) * CAP + slot_rank).astype(jnp.int32)
    gate_flat = gates.reshape(-1)
    x_rows = jnp.zeros((EXPERTS, ROWS, D), jnp.bfloat16).at[expert_of, row_of].set(tokens[token_of])
    weighted = (gate_flat[:, None] * cotangent[token_of].astype(jnp.float32)).astype(jnp.bfloat16)
    dout_rows = jnp.zeros((EXPERTS, ROWS, D), jnp.bfloat16).at[expert_of, row_of].set(weighted)
    out_rows, row_grads, grad_gate, grad_up, grad_down = lax.map(
        expert_work, (x_rows, dout_rows, w_gate, w_up, w_down))
    picked = out_rows[expert_of, row_of].astype(jnp.float32) * gate_flat[:, None]
    mixed = jnp.sum(picked.reshape(TOKENS, TOP, D), axis=1).astype(jnp.bfloat16)
    back = row_grads[expert_of, row_of].astype(jnp.float32)
    input_grad = jnp.sum(back.reshape(TOKENS, TOP, D), axis=1).astype(jnp.bfloat16)
    return mixed, input_grad, grad_gate, grad_up, grad_down
```

```python
import functools

import jax
import jax.numpy as jnp
from jax import lax
from jax.experimental import pallas as pl
from jax.experimental.pallas import tpu as pltpu
from jax.sharding import PartitionSpec as P


BF = jnp.bfloat16
F32 = jnp.float32
CORES = 2


def dot(a, b, ca, cb):
    return lax.dot_general(a, b, (((ca,), (cb,)), ((), ())), preferred_element_type=F32)


def selector(meta, rows):
    place = meta[0:1, :].astype(jnp.int32)
    hit = lax.broadcasted_iota(jnp.int32, (rows, meta.shape[1]), 0) == place
    weight = jnp.sum(jnp.where(hit, meta[1:2, :], 0.0), axis=1, keepdims=True)
    return jnp.where(hit, 1.0, 0.0).astype(BF), weight


def front_body(meta_ref, own_ref, other_ref, wg_ref, wu_ref, wd_ref, *outs, rows, parts):
    x_ref, d_ref = outs[0], outs[1]
    part_refs = outs[2:]

    @pl.when(pl.program_id(0) == 0)
    def _():
        pick, weight = selector(meta_ref[0], rows)
        half = own_ref.shape[1]
        left, right = pick[:, :half], pick[:, half:]
        x = dot(left, own_ref[0], 1, 0) + dot(right, other_ref[0], 1, 0)
        x_ref[...] = x.astype(BF)
        d = dot(left, own_ref[1], 1, 0) + dot(right, other_ref[1], 1, 0)
        d_ref[...] = (d * weight).astype(BF)

    x, d = x_ref[...], d_ref[...]
    values = (
        dot(x, wg_ref[0], 1, 0).astype(BF),
        dot(x, wu_ref[0], 1, 0).astype(BF),
        dot(d, wd_ref[0], 1, 1).astype(BF),
    )
    block = rows // parts
    for r in range(parts):
        for i, v in enumerate(values):
            part_refs[r][i] = v[r * block : (r + 1) * block]


def front(meta, k, own, other, wg, wu, wd, rows, parts):
    tok, feat = own.shape[1:]
    hid = wg.shape[2]
    tile = 256
    block = rows // parts
    whole = pl.BlockSpec((2, tok, feat), lambda i: (0, 0, 0))
    out_shape = [jax.ShapeDtypeStruct((rows, feat), BF)] * 2
    out_shape += [jax.ShapeDtypeStruct((3, block, hid), BF)] * parts
    out_specs = [pl.BlockSpec((rows, feat), lambda i: (0, 0))] * 2
    out_specs += [pl.BlockSpec((3, block, tile), lambda i: (0, 0, i))] * parts
    return pl.pallas_call(
        functools.partial(front_body, rows=rows, parts=parts),
        grid=(hid // tile,),
        in_specs=[
            pl.BlockSpec((1, 2, CORES * tok), lambda i: (k, 0, 0)),
            whole,
            whole,
            pl.BlockSpec((1, feat, tile), lambda i: (0, 0, i)),
            pl.BlockSpec((1, feat, tile), lambda i: (0, 0, i)),
            pl.BlockSpec((1, tile, feat), lambda i: (0, i, 0)),
        ],
        out_specs=out_specs,
        out_shape=out_shape,
        name="front",
        cost_estimate=pl.CostEstimate(
            flops=6 * rows * feat * hid + 4 * rows * CORES * tok * feat,
            bytes_accessed=6 * hid * feat + 8 * tok * feat + 4 * rows * feat + 6 * rows * hid,
            transcendentals=0,
        ),
    )(meta, own, other, wg, wu, wd)


def mid_body(*refs):
    out_ref = refs[-1]
    total = [None] * 3
    for i in range(3):
        acc = refs[0][i].astype(F32)
        for ref in refs[1:-1]:
            acc = acc + ref[i].astype(F32)
        total[i] = acc
    gate, up, grad = total
    sig = jax.nn.sigmoid(gate)
    act = gate * sig
    out_ref[0] = (act * up).astype(BF)
    out_ref[1] = (grad * up * sig * (1.0 + gate * (1.0 - sig))).astype(BF)
    out_ref[2] = (grad * act).astype(BF)


def mid(pieces):
    shape = pieces[0].shape
    size = shape[0] * shape[1] * shape[2]
    return pl.pallas_call(
        mid_body,
        out_shape=jax.ShapeDtypeStruct(shape, BF),
        name="mid",
        cost_estimate=pl.CostEstimate(
            flops=8 * size, bytes_accessed=2 * size * (len(pieces) + 1), transcendentals=size // 3
        ),
    )(*pieces)


def back_body(meta_ref, *refs, rows, parts):
    acts = refs[:parts]
    wg_ref, wu_ref, wd_ref, keep_ref, give_ref, pick_ref, weight_ref, act_ref = refs[parts:]
    block = rows // parts

    @pl.when(pl.program_id(0) == 0)
    def _():
        pick, weight = selector(meta_ref[0], rows)
        pick_ref[...] = pick
        weight_ref[...] = weight
        for r in range(parts):
            for i in range(3):
                act_ref[i, r * block : (r + 1) * block] = acts[r][i]

    pick = pick_ref[...]
    half = pick.shape[1] // CORES
    out = dot(act_ref[0], wd_ref[0], 1, 0).astype(BF).astype(F32)
    out = (out * weight_ref[...]).astype(BF)
    back = dot(act_ref[1], wg_ref[0], 1, 1) + dot(act_ref[2], wu_ref[0], 1, 1)
    back = back.astype(BF)
    for i, v in enumerate((out, back)):
        spread = dot(pick, v, 0, 0).astype(BF)
        keep_ref[i] = spread[:half]
        give_ref[i] = spread[half:]


def back(meta, k, acts, wg, wu, wd, rows, parts):
    hid, feat = wd.shape[1:]
    tok = meta.shape[2] // CORES
    block = rows // parts
    tile = 256
    one = pl.BlockSpec((3, block, hid), lambda i: (0, 0, 0))
    out = pl.BlockSpec((2, tok, tile), lambda i: (0, 0, i))
    return pl.pallas_call(
        functools.partial(back_body, rows=rows, parts=parts),
        grid=(feat // tile,),
        in_specs=[pl.BlockSpec((1, 2, CORES * tok), lambda i: (k, 0, 0))]
        + [one] * parts
        + [
            pl.BlockSpec((1, tile, hid), lambda i: (0, i, 0)),
            pl.BlockSpec((1, tile, hid), lambda i: (0, i, 0)),
            pl.BlockSpec((1, hid, tile), lambda i: (0, 0, i)),
        ],
        out_specs=[out, out],
        out_shape=[jax.ShapeDtypeStruct((2, tok, feat), BF)] * 2,
        scratch_shapes=[
            pltpu.VMEM((rows, CORES * tok), BF),
            pltpu.VMEM((rows, 1), F32),
            pltpu.VMEM((3, rows, hid), BF),
        ],
        name="back",
        cost_estimate=pl.CostEstimate(
            flops=6 * rows * feat * hid + 4 * rows * CORES * tok * feat,
            bytes_accessed=6 * hid * feat + 8 * tok * feat + 6 * rows * hid,
            transcendentals=0,
        ),
    )(meta, *acts, wg, wu, wd)


def weights_body(*refs, chunks, parts, rows):
    xs, ds = refs[:chunks], refs[chunks : 2 * chunks]
    acts = refs[2 * chunks : 2 * chunks + chunks * parts]
    gg_ref, gu_ref, gd_ref, x_ref, d_ref, hid_ref, both_ref = refs[2 * chunks + chunks * parts :]
    block = rows // parts
    hid = hid_ref.shape[1]

    @pl.when(pl.program_id(0) == 0)
    def _():
        for c in range(chunks):
            for r in range(parts):
                at = c * rows + r * block
                ref = acts[c * parts + r]
                hid_ref[at : at + block] = ref[0]
                both_ref[at : at + block, :hid] = ref[1]
                both_ref[at : at + block, hid:] = ref[2]

    for c in range(chunks):
        x_ref[c * rows : (c + 1) * rows] = xs[c][...]
        d_ref[c * rows : (c + 1) * rows] = ds[c][...]
    pair = dot(x_ref[...], both_ref[...], 0, 0).astype(BF)
    gg_ref[0] = pair[:, :hid]
    gu_ref[0] = pair[:, hid:]
    gd_ref[0] = dot(hid_ref[...], d_ref[...], 0, 0).astype(BF)


def weight_grads(xs, ds, acts, rows, parts, hid):
    chunks = len(xs)
    feat = xs[0].shape[1]
    block = rows // parts
    tile = 256
    row_spec = pl.BlockSpec((rows, tile), lambda i: (0, i))
    act_spec = pl.BlockSpec((3, block, hid), lambda i: (0, 0, 0))
    flat = [a for chunk in acts for a in chunk]
    return pl.pallas_call(
        functools.partial(weights_body, chunks=chunks, parts=parts, rows=rows),
        grid=(feat // tile,),
        in_specs=[row_spec] * (2 * chunks) + [act_spec] * len(flat),
        out_specs=[
            pl.BlockSpec((1, tile, hid), lambda i: (0, i, 0)),
            pl.BlockSpec((1, tile, hid), lambda i: (0, i, 0)),
            pl.BlockSpec((1, hid, tile), lambda i: (0, 0, i)),
        ],
        out_shape=[
            jax.ShapeDtypeStruct((1, feat, hid), BF),
            jax.ShapeDtypeStruct((1, feat, hid), BF),
            jax.ShapeDtypeStruct((1, hid, feat), BF),
        ],
        scratch_shapes=[
            pltpu.VMEM((chunks * rows, tile), BF),
            pltpu.VMEM((chunks * rows, tile), BF),
            pltpu.VMEM((chunks * rows, hid), BF),
            pltpu.VMEM((chunks * rows, 2 * hid), BF),
        ],
        name="weight_grads",
        cost_estimate=pl.CostEstimate(
            flops=6 * chunks * rows * feat * hid,
            bytes_accessed=6 * hid * feat + chunks * rows * (4 * feat + 6 * hid),
            transcendentals=0,
        ),
    )(*xs, *ds, *flat)


def local(tokens, cotangent, routes, gates, w_gate, w_up, w_down):
    tok, feat = tokens.shape
    picks = routes.shape[1]
    experts = lax.axis_size("expert")
    parts = lax.axis_size("dp")
    chips = experts // CORES
    hid = w_gate.shape[2]
    capacity = 3 * tok * picks // (2 * experts)
    unit = 16 * parts
    rows = (CORES * capacity + unit - 1) // unit * unit
    block = rows // parts

    def ring(step):
        return [(i, (i + CORES * step) % experts) for i in range(experts)]

    def hop(a, step):
        return lax.ppermute(a, "expert", ring(step))

    def swap(a):
        return lax.ppermute(a, "expert", [(i, i ^ 1) for i in range(experts)])

    def across(a, r):
        return lax.ppermute(a, "dp", [(i, i ^ r) for i in range(parts)])

    mine = jnp.stack([tokens, cotangent])
    near = chips // 2
    got = {0: mine}
    for k in range(1, near + 1):
        got[k] = hop(got[k - 1], 1)
        j = chips - k
        if j > near:
            got[j] = hop(got[(j + 1) % chips], -1)

    named = routes[:, :, None] == jnp.arange(experts, dtype=jnp.int32)[None, None, :]
    member = jnp.any(named, axis=1)
    gate_of = jnp.sum(jnp.where(named, gates[:, :, None], 0.0), axis=1)
    earlier = jnp.tril(jnp.ones((tok, tok), BF), -1)
    slot = jnp.dot(earlier, member.astype(BF), preferred_element_type=F32)
    slot = jnp.where(member, slot, -1.0)
    sent = jnp.stack([slot.T, gate_of.T], axis=1)
    meta = lax.all_to_all(sent, "expert", split_axis=0, concat_axis=0, tiled=True)

    me = lax.axis_index("expert")
    chip, core = me // CORES, me % CORES
    order = jnp.arange(experts, dtype=jnp.int32)
    source = ((chip - order // CORES) % chips) * CORES + (core ^ (order % CORES))
    chosen = source[:, None] == order[None, :]
    meta = jnp.sum(jnp.where(chosen[:, :, None, None], meta[None], 0.0), axis=1)
    slot = meta[:, 0].astype(jnp.int32)
    row = slot + (order % CORES)[:, None] * capacity
    row = ((row // block) ^ lax.axis_index("dp")) * block + row % block
    row = jnp.where(slot < 0, -1, row).astype(F32)
    meta = jnp.stack([row.reshape(chips, -1), meta[:, 1].reshape(chips, -1)], axis=1)

    sequence = [0]
    for k in range(1, near + 1):
        sequence.append(k)
        if chips - k > near:
            sequence.append(chips - k)
    sequence = sorted(sequence, key=lambda k: (k == near, sequence.index(k)))

    xs, ds, acts, sums = {}, {}, {}, {}
    for k in sequence:
        other = swap(got[k])
        xs[k], ds[k], *pieces = front(meta, k, got[k], other, w_gate, w_up, w_down, rows, parts)
        pieces = [pieces[0]] + [across(pieces[r], r) for r in range(1, parts)]
        act = mid(pieces)
        acts[k] = [act] + [across(act, r) for r in range(1, parts)]
        keep, give = back(meta, k, acts[k], w_gate, w_up, w_down, rows, parts)
        taken = swap(give)
        if k == 0:
            sums[k] = [keep, taken]
        else:
            total = (keep.astype(F32) + taken.astype(F32)).astype(BF)
            sums[k] = [lax.ppermute(total, "expert", ring(-k))]
    grads = weight_grads(
        [xs[k] for k in sequence],
        [ds[k] for k in sequence],
        [acts[k] for k in sequence],
        rows,
        parts,
        hid,
    )
    final = sum(a.astype(F32) for k in sequence for a in sums[k]).astype(BF)
    return (final[0], final[1], *grads)


def solution(mesh):
    in_specs = (
        P("expert", "dp"),
        P("expert", "dp"),
        P("expert", None),
        P("expert", None),
        P("expert", "dp", None),
        P("expert", "dp", None),
        P("expert", None, "dp"),
    )
    out_specs = (
        P("expert", "dp"),
        P("expert", "dp"),
        P("expert", "dp", None),
        P("expert", "dp", None),
        P("expert", None, "dp"),
    )
    return jax.shard_map(local, mesh=mesh, in_specs=in_specs, out_specs=out_specs, check_vma=False)
```

```python
import functools

import jax
import jax.numpy as jnp
from jax import lax
from jax.experimental import pallas as pl
from jax.experimental.pallas import tpu as pltpu
from jax.sharding import PartitionSpec as P


BF = jnp.bfloat16
F32 = jnp.float32
CORES = 2
LIMIT = pltpu.CompilerParams(vmem_limit_bytes=24 * 1024 * 1024)


def dot(a, b, ca, cb):
    return lax.dot_general(a, b, (((ca,), (cb,)), ((), ())), preferred_element_type=F32)


def pack_body(tok_ref, cot_ref, routes_ref, gates_ref, out_ref, *, experts):
    tok, feat = tok_ref.shape
    picks = routes_ref.shape[0]
    lanes = out_ref.shape[1] - 2 * feat
    out_ref[:, :feat] = tok_ref[...]
    out_ref[:, feat : 2 * feat] = cot_ref[...]
    gates = gates_ref[...]
    high = gates.astype(BF).astype(F32)
    middle = (gates - high).astype(BF).astype(F32)
    low = gates - high - middle
    pieces = jnp.concatenate([routes_ref[...].astype(F32), high, middle, low], axis=0)
    at, to = (lax.broadcasted_iota(jnp.int32, (tok, tok), d) for d in (0, 1))
    turned = dot(jnp.where(at == to, 1.0, 0.0).astype(BF), pieces.astype(BF), 1, 1)
    lane = lax.broadcasted_iota(jnp.int32, (tok, lanes), 1)
    expert, kind = (lane % experts).astype(F32), lane // experts
    member = jnp.zeros((tok, lanes), F32)
    value = jnp.zeros((tok, lanes), F32)
    for k in range(picks):
        hit = turned[:, k : k + 1] == expert
        member = member + jnp.where(hit, 1.0, 0.0)
        for piece in range(1, 4):
            column = turned[:, piece * picks + k : piece * picks + k + 1]
            value = jnp.where(hit & (kind == piece), column, value)
    slot = dot(jnp.where(to < at, 1.0, 0.0).astype(BF), member.astype(BF), 1, 0)
    value = jnp.where(kind == 0, jnp.where(member > 0.0, slot, -1.0), value)
    out_ref[:, 2 * feat :] = value.astype(BF)


def pack(tokens, cotangent, routes, gates, experts):
    tok, feat = tokens.shape
    lanes = (4 * experts + 127) // 128 * 128
    return pl.pallas_call(
        functools.partial(pack_body, experts=experts),
        out_shape=jax.ShapeDtypeStruct((tok, 2 * feat + lanes), BF),
        name="pack",
        compiler_params=LIMIT,
    )(tokens, cotangent, routes.T, gates.T)


def columns(experts, lanes):
    mine = lax.axis_index("expert")
    lane = lax.broadcasted_iota(jnp.int32, (8, lanes), 1)
    want = lax.broadcasted_iota(jnp.int32, (8, lanes), 0)
    return jnp.where((lane % experts == mine) & (lane // experts == want), 1.0, 0.0).astype(BF)


def places(slot, block, parts):
    slot = slot.astype(jnp.int32)
    mine = lax.axis_index("dp") % (parts // CORES)
    return jnp.where(slot < 0, -1, ((slot // block) ^ mine) * block + slot % block)


def front_body(own_ref, other_ref, wg_ref, wu_ref, wd_ref, *outs, rows, parts, experts):
    x_ref, d_ref, meta_ref = outs[:3]
    part_refs = outs[3:]
    block = rows // parts

    @pl.when(pl.program_id(0) == 0)
    def _():
        tok = own_ref.shape[0]
        feat, half = x_ref.shape[1], rows // CORES
        lanes = own_ref.shape[1] - 2 * feat
        swapped = lax.axis_index("dp") >= parts // CORES
        take = columns(experts, lanes)
        for h, (a_ref, b_ref) in enumerate(((own_ref, other_ref), (other_ref, own_ref))):
            meta = jnp.where(swapped, b_ref[:, 2 * feat :], a_ref[:, 2 * feat :])
            meta_ref[h] = meta
            row = dot(take, meta, 1, 1)
            place = places(row[0:1], block, parts)
            hit = lax.broadcasted_iota(jnp.int32, (half, tok), 0) == place
            gate = (row[1:2] + row[2:3]) + row[3:4]
            gate = jnp.sum(jnp.where(hit, gate, 0.0), axis=1, keepdims=True)
            pick = jnp.where(hit, 1.0, 0.0).astype(BF)
            x = jnp.where(swapped, b_ref[:, :feat], a_ref[:, :feat])
            x_ref[h * half : (h + 1) * half] = dot(pick, x, 1, 0).astype(BF)
            d = jnp.where(swapped, b_ref[:, feat : 2 * feat], a_ref[:, feat : 2 * feat])
            d_ref[h * half : (h + 1) * half] = (dot(pick, d, 1, 0) * gate).astype(BF)

    x, d = x_ref[...], d_ref[...]
    values = (
        dot(x, wg_ref[0], 1, 0).astype(BF),
        dot(x, wu_ref[0], 1, 0).astype(BF),
        dot(d, wd_ref[0], 1, 1).astype(BF),
    )
    for r in range(parts):
        for i, v in enumerate(values):
            part_refs[r][i] = v[r * block : (r + 1) * block]


def front(own, other, wg, wu, wd, rows, parts, experts):
    tok, wide = own.shape
    feat, hid = wg.shape[1:]
    tile = 256
    block = rows // parts
    whole = pl.BlockSpec((tok, wide), lambda i: (0, 0))
    out_shape = [jax.ShapeDtypeStruct((rows, feat), BF)] * 2
    out_shape += [jax.ShapeDtypeStruct((CORES, tok, wide - 2 * feat), BF)]
    out_shape += [jax.ShapeDtypeStruct((3, block, hid), BF)] * parts
    out_specs = [pl.BlockSpec((rows, feat), lambda i: (0, 0))] * 2
    out_specs += [pl.BlockSpec((CORES, tok, wide - 2 * feat), lambda i: (0, 0, 0))]
    out_specs += [pl.BlockSpec((3, block, tile), lambda i: (0, 0, i))] * parts
    return pl.pallas_call(
        functools.partial(front_body, rows=rows, parts=parts, experts=experts),
        grid=(hid // tile,),
        in_specs=[
            whole,
            whole,
            pl.BlockSpec((1, feat, tile), lambda i: (0, 0, i)),
            pl.BlockSpec((1, feat, tile), lambda i: (0, 0, i)),
            pl.BlockSpec((1, tile, feat), lambda i: (0, i, 0)),
        ],
        out_specs=out_specs,
        out_shape=out_shape,
        name="front",
        compiler_params=LIMIT,
        cost_estimate=pl.CostEstimate(
            flops=6 * rows * feat * hid + 4 * rows * tok * feat,
            bytes_accessed=6 * hid * feat + 8 * tok * feat + 4 * rows * feat + 6 * rows * hid,
            transcendentals=0,
        ),
    )(own, other, wg, wu, wd)


def mid_body(*refs):
    out_ref = refs[-1]
    total = [None] * 3
    for i in range(3):
        acc = refs[0][i].astype(F32)
        for ref in refs[1:-1]:
            acc = acc + ref[i].astype(F32)
        total[i] = acc
    gate, up, grad = total
    sig = jax.nn.sigmoid(gate)
    act = gate * sig
    out_ref[0] = (act * up).astype(BF)
    out_ref[1] = (grad * up * sig * (1.0 + gate * (1.0 - sig))).astype(BF)
    out_ref[2] = (grad * act).astype(BF)


def mid(pieces):
    shape = pieces[0].shape
    size = shape[0] * shape[1] * shape[2]
    return pl.pallas_call(
        mid_body,
        out_shape=jax.ShapeDtypeStruct(shape, BF),
        name="mid",
        compiler_params=LIMIT,
        cost_estimate=pl.CostEstimate(
            flops=8 * size, bytes_accessed=2 * size * (len(pieces) + 1), transcendentals=size // 3
        ),
    )(*pieces)


def back_body(meta_ref, *refs, rows, parts, experts):
    acts = refs[:parts]
    wg_ref, wu_ref, wd_ref, keep_ref, give_ref, pick_ref, gate_ref, act_ref = refs[parts:]
    block = rows // parts
    half = rows // CORES

    @pl.when(pl.program_id(0) == 0)
    def _():
        take = columns(experts, meta_ref.shape[2])
        for h in range(CORES):
            col = dot(meta_ref[h], take, 1, 1)
            place = places(col[:, 0:1], block, parts)
            hit = lax.broadcasted_iota(jnp.int32, (place.shape[0], half), 1) == place
            pick_ref[h] = jnp.where(hit, 1.0, 0.0).astype(BF)
            gate_ref[h] = (col[:, 1:2] + col[:, 2:3]) + col[:, 3:4]
        for r in range(parts):
            for i in range(3):
                act_ref[i, r * block : (r + 1) * block] = acts[r][i]

    swapped = lax.axis_index("dp") >= parts // CORES
    out = dot(act_ref[0], wd_ref[0], 1, 0).astype(BF)
    back = (dot(act_ref[1], wg_ref[0], 1, 1) + dot(act_ref[2], wu_ref[0], 1, 1)).astype(BF)
    first, second = (slice(0, half), slice(half, rows))
    mixed = [
        (dot(pick_ref[h], out[s], 1, 0) * gate_ref[h]).astype(BF)
        for h, s in enumerate((first, second))
    ]
    grad = [dot(pick_ref[h], back[s], 1, 0).astype(BF) for h, s in enumerate((first, second))]
    for i, (a, b) in enumerate((mixed, grad)):
        keep_ref[i] = jnp.where(swapped, b, a)
        give_ref[i] = jnp.where(swapped, a, b)


def back(meta, acts, wg, wu, wd, rows, parts, experts):
    hid, feat = wd.shape[1:]
    tok = meta.shape[1]
    block = rows // parts
    tile = 256
    one = pl.BlockSpec((3, block, hid), lambda i: (0, 0, 0))
    out = pl.BlockSpec((2, tok, tile), lambda i: (0, 0, i))
    return pl.pallas_call(
        functools.partial(back_body, rows=rows, parts=parts, experts=experts),
        grid=(feat // tile,),
        in_specs=[pl.BlockSpec(meta.shape, lambda i: (0, 0, 0))]
        + [one] * parts
        + [
            pl.BlockSpec((1, tile, hid), lambda i: (0, i, 0)),
            pl.BlockSpec((1, tile, hid), lambda i: (0, i, 0)),
            pl.BlockSpec((1, hid, tile), lambda i: (0, 0, i)),
        ],
        out_specs=[out, out],
        out_shape=[jax.ShapeDtypeStruct((2, tok, feat), BF)] * 2,
        scratch_shapes=[
            pltpu.VMEM((CORES, tok, rows // CORES), BF),
            pltpu.VMEM((CORES, tok, 1), F32),
            pltpu.VMEM((3, rows, hid), BF),
        ],
        name="back",
        compiler_params=LIMIT,
        cost_estimate=pl.CostEstimate(
            flops=6 * rows * feat * hid + 4 * rows * tok * feat,
            bytes_accessed=6 * hid * feat + 8 * tok * feat + 6 * rows * hid,
            transcendentals=0,
        ),
    )(meta, *acts, wg, wu, wd)


def weights_body(*refs, chunks, parts, rows):
    xs, ds = refs[:chunks], refs[chunks : 2 * chunks]
    acts = refs[2 * chunks : 2 * chunks + chunks * parts]
    gg_ref, gu_ref, gd_ref, x_ref, d_ref, hid_ref, both_ref = refs[2 * chunks + chunks * parts :]
    block = rows // parts
    hid = hid_ref.shape[1]

    @pl.when(pl.program_id(0) == 0)
    def _():
        for c in range(chunks):
            for r in range(parts):
                at = c * rows + r * block
                ref = acts[c * parts + r]
                hid_ref[at : at + block] = ref[0]
                both_ref[at : at + block, :hid] = ref[1]
                both_ref[at : at + block, hid:] = ref[2]

    for c in range(chunks):
        x_ref[c * rows : (c + 1) * rows] = xs[c][...]
        d_ref[c * rows : (c + 1) * rows] = ds[c][...]
    pair = dot(x_ref[...], both_ref[...], 0, 0).astype(BF)
    gg_ref[0] = pair[:, :hid]
    gu_ref[0] = pair[:, hid:]
    gd_ref[0] = dot(hid_ref[...], d_ref[...], 0, 0).astype(BF)


def weight_grads(xs, ds, acts, rows, parts, hid):
    chunks = len(xs)
    feat = xs[0].shape[1]
    block = rows // parts
    tile = 256
    row_spec = pl.BlockSpec((rows, tile), lambda i: (0, i))
    act_spec = pl.BlockSpec((3, block, hid), lambda i: (0, 0, 0))
    flat = [a for chunk in acts for a in chunk]
    return pl.pallas_call(
        functools.partial(weights_body, chunks=chunks, parts=parts, rows=rows),
        grid=(feat // tile,),
        in_specs=[row_spec] * (2 * chunks) + [act_spec] * len(flat),
        out_specs=[
            pl.BlockSpec((1, tile, hid), lambda i: (0, i, 0)),
            pl.BlockSpec((1, tile, hid), lambda i: (0, i, 0)),
            pl.BlockSpec((1, hid, tile), lambda i: (0, 0, i)),
        ],
        out_shape=[
            jax.ShapeDtypeStruct((1, feat, hid), BF),
            jax.ShapeDtypeStruct((1, feat, hid), BF),
            jax.ShapeDtypeStruct((1, hid, feat), BF),
        ],
        scratch_shapes=[
            pltpu.VMEM((chunks * rows, tile), BF),
            pltpu.VMEM((chunks * rows, tile), BF),
            pltpu.VMEM((chunks * rows, hid), BF),
            pltpu.VMEM((chunks * rows, 2 * hid), BF),
        ],
        name="weight_grads",
        compiler_params=LIMIT,
        cost_estimate=pl.CostEstimate(
            flops=6 * chunks * rows * feat * hid,
            bytes_accessed=6 * hid * feat + chunks * rows * (4 * feat + 6 * hid),
            transcendentals=0,
        ),
    )(*xs, *ds, *flat)


def final_body(*refs):
    for i in range(2):
        total = refs[0][i].astype(F32)
        for ref in refs[1:-2]:
            total = total + ref[i].astype(F32)
        refs[-2 + i][...] = total.astype(BF)


def final(arrays):
    return pl.pallas_call(
        final_body,
        out_shape=[jax.ShapeDtypeStruct(arrays[0].shape[1:], BF)] * 2,
        name="final",
        compiler_params=LIMIT,
    )(*arrays)


def local(tokens, cotangent, routes, gates, w_gate, w_up, w_down):
    tok, _ = tokens.shape
    picks = routes.shape[1]
    experts = lax.axis_size("expert")
    parts = lax.axis_size("dp")
    chips = experts // CORES
    hid = w_gate.shape[2]
    capacity = 3 * tok * picks // (2 * experts)
    unit = 16 * parts // CORES
    rows = CORES * ((capacity + unit - 1) // unit * unit)

    def ring(step):
        return [(i, (i + CORES * step) % experts) for i in range(experts)]

    def hop(a, step):
        return lax.ppermute(a, "expert", ring(step))

    def swap(a):
        return lax.ppermute(a, "expert", [(i, i ^ 1) for i in range(experts)])

    def across(a, r):
        return lax.ppermute(a, "dp", [(i, i ^ r) for i in range(parts)])

    near = chips // 2
    got = {0: pack(tokens, cotangent, routes, gates, experts)}
    sequence = [0]
    for k in range(1, near + 1):
        got[k] = hop(got[k - 1], 1)
        sequence.append(k)
        j = chips - k
        if j > near:
            got[j] = hop(got[(j + 1) % chips], -1)
            sequence.append(j)
    sequence.sort(key=lambda k: min(k, chips - k))

    xs, ds, acts, sums = {}, {}, {}, {}
    for k in sequence:
        other = swap(got[k])
        xs[k], ds[k], meta, *pieces = front(
            got[k], other, w_gate, w_up, w_down, rows, parts, experts
        )
        pieces = [pieces[0]] + [across(pieces[r], r) for r in range(1, parts)]
        act = mid(pieces)
        acts[k] = [act] + [across(act, r) for r in range(1, parts)]
        keep, give = back(meta, acts[k], w_gate, w_up, w_down, rows, parts, experts)
        sums[k] = [keep, swap(give)]

    back_home = list(sums[0])
    for chain, step in ((range(near - 1, 0, -1), -1), (range(near, chips), 1)):
        carried = []
        for k in chain:
            total = sum(a.astype(F32) for a in sums[k] + carried).astype(BF)
            carried = [hop(total, step)]
        back_home += carried
    grads = weight_grads(
        [xs[k] for k in sequence],
        [ds[k] for k in sequence],
        [acts[k] for k in sequence],
        rows,
        parts,
        hid,
    )
    mixed, input_grad = final(back_home)
    return (mixed, input_grad, *grads)


def solution(mesh):
    in_specs = (
        P("expert", "dp"),
        P("expert", "dp"),
        P("expert", None),
        P("expert", None),
        P("expert", "dp", None),
        P("expert", "dp", None),
        P("expert", None, "dp"),
    )
    out_specs = (
        P("expert", "dp"),
        P("expert", "dp"),
        P("expert", "dp", None),
        P("expert", "dp", None),
        P("expert", None, "dp"),
    )

    return jax.shard_map(local, mesh=mesh, in_specs=in_specs, out_specs=out_specs, check_vma=False)
```
